32 devices in a mesh: seq: 16 (over z, y, core), dp: 2 (over x).
Axes of the slice: x: 2, y: 2, z: 4, core: 2. Of those that a mesh axis runs over, the one named last changes fastest.
Arguments:
- queries: bfloat16 [2, 2048, 2048], P('dp', 'seq'), may hold values from -8 to 8
- keys: bfloat16 [2, 2048, 1024], P('dp', 'seq'), may hold values from -8 to 8
- values: bfloat16 [2, 2048, 1024], P('dp', 'seq'), may hold values from -6 to 6
- segments: int32 [2, 2048], P('dp', 'seq'), may hold values from 0 to 3, never falling along the last dimension, each value on 1 to 1024 neighbouring positions
- q_gain: float32 [128], replicated, may hold values from 0.5 to 6
- k_gain: float32 [128], replicated, may hold values from 0.5 to 6
- d_attn: bfloat16 [2, 2048, 2048], P('dp', 'seq'), may hold values from -6 to 6
Outputs:
- attn_out: bfloat16 [2, 2048, 2048], P('dp', 'seq')
- grad_queries: bfloat16 [2, 2048, 2048], P('dp', 'seq')
- grad_keys: bfloat16 [2, 2048, 1024], P('dp', 'seq')
- grad_values: bfloat16 [2, 2048, 1024], P('dp', 'seq')
- gain_grads: float32 [2, 128], replicated
The draws below stay inside these ranges and needn't reach their ends.
All inputs are finite; a program needn't handle non-finite values.
Results may differ from the reference program's by a relative error of at most 0.0065.
The reference program's roundings to bfloat16 on the way (of `q_norm`, `k_norm`, `prob_low` and `grad_score`) count: a program that leaves them out, or rounds other values in their place, can miss the bound.
Values may be sent and summed in bfloat16 or wider, within the bound.
A program may use at most 64 MiB of HBM per device.

```python
import math
import jax
import jax.numpy as jnp
import numpy as np
from jax import lax

HD = 128
QH = 16
KVH = 8
QPA = 168
WINDOW = 256
ROWS = 128
SEQS = 2
LEN = 2048
N_SEQ = 16


def shared_pair(key):
    key = jax.random.fold_in(key, 7)
    q_key, k_key = jax.random.split(key, 2)
    query_rows = jax.random.truncated_normal(q_key, -6.0, 6.0, (SEQS, LEN, QH, HD), jnp.float32)
    key_rows = jax.random.truncated_normal(k_key, -6.0, 6.0, (SEQS, LEN, KVH, HD), jnp.float32)
    return (query_rows.reshape(SEQS, LEN, QH * HD), key_rows.reshape(SEQS, LEN, KVH * HD))


def draw_queries(key, part):
    return shared_pair(key)[0].astype(jnp.bfloat16)


def draw_keys(key, part):
    return shared_pair(key)[1].astype(jnp.bfloat16)


def gain_law(key):
    gains = jax.random.uniform(key, (HD,), jnp.float32, 0.6, 1.6)
    return gains


def draw_q_gain(key, part):
    return gain_law(jax.random.fold_in(key, 31))


def draw_k_gain(key, part):
    return gain_law(jax.random.fold_in(key, 37))


def level_of(stream_key, shape, cuts, least, top_value):
    def one(position, shards_of):
        steps = jax.random.uniform(jax.random.fold_in(jax.random.fold_in(stream_key, 6), position), (shards_of,), jnp.float32, least / len(cuts), top_value / len(cuts))
        return jnp.repeat(jnp.exp(steps), shape[position] // shards_of).reshape((-1,) + (1,) * (len(shape) - position - 1))

    level = one(*cuts[0])
    for cut in cuts[1:]:
        level = level * one(*cut)
    return level


def split_up(amount, total, limit, skew):
    portions = [(1 << 20) // math.isqrt(standing ** skew) + 1 for standing in range(2, amount + 1)]
    surplus, given = total - limit - (amount - 1), [1] * (amount - 1)
    while surplus > 0:
        movable = [i for i in range(amount - 1) if given[i] < limit]
        pool, remaining = sum([portions[i] for i in movable]), surplus
        for i in movable:
            more = min(limit - given[i], max(1, remaining * portions[i] // pool), surplus)
            given[i] = given[i] + more
            surplus = surplus - more
    return np.array([limit] + given)


def ragged_sizes(own_key, number_of, total, reach, lean):
    if number_of == 2:
        one = jax.random.randint(own_key, (), max(1, total - reach), min(reach, total - 1) + 1)
        return jnp.stack([one, total - one])
    tallies = jnp.asarray(split_up(number_of, total, reach, lean), jnp.int32)
    couples = (number_of - 1) // 2
    giver, taker = tallies[1:1 + 2 * couples:2], tallies[2:2 + 2 * couples:2]
    slack = jnp.minimum(giver - 1, reach - taker)
    moved = jax.random.randint(jax.random.fold_in(own_key, 1), (couples,), 0, 1 << 20) % (slack + 1)
    tallies = tallies.at[1:1 + 2 * couples:2].set(giver - moved).at[2:2 + 2 * couples:2].set(taker + moved)
    return tallies[jax.random.permutation(jax.random.fold_in(own_key, 2), number_of)]


def gaussian(key, dims, width, reach, shards=(), kind=jnp.bfloat16):
    entries = width * jax.random.normal(key, dims, jnp.float32)
    if shards:
        entries = entries * level_of(key, dims, shards, -0.22, 0.18)
    return jnp.clip(entries, -reach, reach).astype(kind)


def setup_inputs(seed: int = 0) -> dict:
    key_of = jax.random.split(jax.random.key(seed), 8)
    return {
        "queries": draw_queries(jax.random.fold_in(key_of[7], 71), 0),
        "keys": draw_keys(jax.random.fold_in(key_of[7], 71), 0),
        "values": gaussian(key_of[2], (SEQS, LEN, KVH * HD), 1.0, 6.0, ((0, 2), (1, 16))),
        "segments": jax.vmap(lambda own: jnp.searchsorted(jnp.cumsum(ragged_sizes(own, N_SEQ // 4, LEN, LEN // 2, 1)), jnp.arange(LEN), side="right"))(jax.random.split(key_of[3], SEQS)).reshape((SEQS, LEN)).astype(jnp.int32),
        "q_gain": draw_q_gain(jax.random.fold_in(key_of[7], 71), 0),
        "k_gain": draw_k_gain(jax.random.fold_in(key_of[7], 71), 0),
        "d_attn": gaussian(key_of[6], (SEQS, LEN, QH * HD), 1.0, 6.0, ((0, 2), (1, 16))),
    }


epsilon = 1e-06

def norm_rows(raw, gain):
    values_f = raw.astype(jnp.float32)
    rms = jnp.sqrt(lax.optimization_barrier(jnp.mean(values_f * values_f, axis=-1, keepdims=True)) + epsilon)
    unit = values_f / rms
    return ((unit * gain).astype(jnp.bfloat16), unit, rms)

def norm_back(grad_norm, unit, rms, gain):
    scaled = grad_norm * gain
    return (scaled - unit * lax.optimization_barrier(jnp.mean(scaled * unit, axis=-1, keepdims=True))) / rms

def one_sequence(packed, q_gain, k_gain):
    q_raw, k_raw, v_raw, doc_ids, cot_raw = packed
    group = QH // KVH
    score_scale = QPA ** (-0.5)
    span = WINDOW + ROWS
    q_norm, q_unit, q_rms = norm_rows(q_raw.reshape(LEN, QH, HD), q_gain)
    k_norm, k_unit, k_rms = norm_rows(k_raw.reshape(LEN, KVH, HD), k_gain)
    q_grouped = q_norm.reshape(LEN, KVH, group, HD)
    cotan = cot_raw.reshape(LEN, KVH, group, HD)
    k_pad = jnp.concatenate([jnp.zeros((WINDOW, KVH, HD), jnp.bfloat16), k_norm], axis=0)
    v_pad = jnp.concatenate([jnp.zeros((WINDOW, KVH, HD), jnp.bfloat16), v_raw.reshape(LEN, KVH, HD)], axis=0)
    doc_pad = jnp.concatenate([jnp.full((WINDOW,), -1, jnp.int32), doc_ids.astype(jnp.int32)])

    def block_step(carry, block):
        k_acc, v_acc = carry
        start = (block * ROWS).astype(jnp.int32)
        q_blk = lax.dynamic_slice_in_dim(q_grouped, start, ROWS, 0).astype(jnp.float32)
        c_blk = lax.dynamic_slice_in_dim(cotan, start, ROWS, 0).astype(jnp.float32)
        k_blk = lax.dynamic_slice_in_dim(k_pad, start, span, 0).astype(jnp.float32)
        v_blk = lax.dynamic_slice_in_dim(v_pad, start, span, 0).astype(jnp.float32)
        doc_q = lax.dynamic_slice_in_dim(doc_ids.astype(jnp.int32), start, ROWS, 0)
        doc_k = lax.dynamic_slice_in_dim(doc_pad, start, span, 0)
        q_pos = start + jnp.arange(ROWS, dtype=jnp.int32)[:, None]
        k_pos = start - WINDOW + jnp.arange(span, dtype=jnp.int32)[None, :]
        allowed = (k_pos <= q_pos) & (q_pos - k_pos < WINDOW) & (doc_q[:, None] == doc_k[None, :])
        scores = jnp.einsum('rhgd,khd->hgrk', q_blk, k_blk) * score_scale
        scores = jnp.where(allowed, scores, -1e+30)
        row_max = lax.optimization_barrier(jnp.max(scores, axis=-1, keepdims=True))
        exp_scores = jnp.exp(scores - row_max)
        attn_prob = exp_scores / lax.optimization_barrier(jnp.sum(exp_scores, axis=-1, keepdims=True))
        prob_low = attn_prob.astype(jnp.bfloat16)
        prob_f = prob_low.astype(jnp.float32)
        out = jnp.einsum('hgrk,khd->rhgd', prob_f, v_blk).astype(jnp.bfloat16)
        grad_prob = jnp.einsum('rhgd,khd->hgrk', c_blk, v_blk)
        row_dots = lax.optimization_barrier(jnp.sum(attn_prob * grad_prob, axis=-1, keepdims=True))
        grad_score = (attn_prob * (grad_prob - row_dots) * score_scale).astype(jnp.bfloat16).astype(jnp.float32)
        grad_q = jnp.einsum('hgrk,khd->rhgd', grad_score, k_blk)
        grad_k = jnp.einsum('hgrk,rhgd->khd', grad_score, q_blk)
        grad_v = jnp.einsum('hgrk,rhgd->khd', prob_f, c_blk)
        k_acc = lax.dynamic_update_slice_in_dim(k_acc, lax.dynamic_slice_in_dim(k_acc, start, span, 0) + grad_k, start, 0)
        v_acc = lax.dynamic_update_slice_in_dim(v_acc, lax.dynamic_slice_in_dim(v_acc, start, span, 0) + grad_v, start, 0)
        return ((k_acc, v_acc), (out, grad_q))
    zeros_acc = jnp.zeros((LEN + WINDOW, KVH, HD), jnp.float32)
    (k_acc, v_acc), (outs, grad_qs) = lax.scan(block_step, (zeros_acc, zeros_acc), jnp.arange(LEN // ROWS, dtype=jnp.int32))
    attn_out = outs.reshape(LEN, QH * HD)
    grad_q = grad_qs.reshape(LEN, QH, HD)
    grad_k = k_acc[WINDOW:]
    grad_v = v_acc[WINDOW:]
    grad_queries = norm_back(grad_q, q_unit, q_rms, q_gain).astype(jnp.bfloat16).reshape(LEN, QH * HD)
    grad_keys = norm_back(grad_k, k_unit, k_rms, k_gain).astype(jnp.bfloat16).reshape(LEN, KVH * HD)
    grad_values = grad_v.astype(jnp.bfloat16).reshape(LEN, KVH * HD)
    q_term = lax.optimization_barrier(jnp.sum(grad_q * q_unit, axis=(0, 1)))
    k_term = lax.optimization_barrier(jnp.sum(grad_k * k_unit, axis=(0, 1)))
    return (attn_out, grad_queries, grad_keys, grad_values, q_term, k_term)

def reference(queries, keys, values, segments, q_gain, k_gain, d_attn):
    results = lax.map(lambda packed: one_sequence(packed, q_gain, k_gain), (queries, keys, values, segments, d_attn))
    attn_out, grad_queries, grad_keys, grad_values, q_terms, k_terms = results
    gain_grads = jnp.stack([lax.optimization_barrier(jnp.sum(q_terms, axis=0)), lax.optimization_barrier(jnp.sum(k_terms, axis=0))]) * (SEQS * LEN) ** (-0.5)
    return (attn_out, grad_queries, grad_keys, grad_values, gain_grads)
```

```python
import functools
import math

import jax
import jax.numpy as jnp
from jax import lax
from jax.experimental import pallas as pl
from jax.experimental.pallas import tpu as pltpu
from jax.sharding import PartitionSpec as P

QPA = 168
WINDOW = 256
HD = 128
EPS = 1e-06
SCALE = QPA ** (-0.5)
EXP2_SCALE = SCALE * math.log2(math.e)
F32 = jnp.float32
BF16 = jnp.bfloat16


def dot(a, b, ca, cb):
    return lax.dot_general(a, b, (((ca,), (cb,)), ((), ())), preferred_element_type=F32)


def inv_rms(x):
    return 1.0 / jnp.sqrt(jnp.mean(x * x, axis=-1, keepdims=True) + EPS)


def stack_heads(x):
    return jnp.concatenate([x[:, :HD], x[:, HD:]], axis=0)


def norm_back(grad, unit, inv, gain):
    t = grad * gain
    return (t - unit * jnp.mean(t * unit, axis=-1, keepdims=True)) * inv


def unit_step(q_raw, c_raw, kn, v, bias02, bias1, low, q_gain):
    x = stack_heads(q_raw).astype(F32)
    c = stack_heads(c_raw)
    inv = inv_rms(x)
    unit = x * inv
    qn = (unit * q_gain).astype(BF16)
    s = dot(qn, kn, 1, 1)
    gp = dot(c, v, 1, 1)
    n = HD
    x02 = jnp.where(low, s[:, 2 * n:], s[:, :n]) + bias02
    x1 = s[:, n:2 * n] + bias1
    m = jnp.max(jnp.maximum(x02, x1), axis=-1, keepdims=True)
    e02 = jnp.exp2((x02 - m) * EXP2_SCALE)
    e1 = jnp.exp2((x1 - m) * EXP2_SCALE)
    il = 1.0 / jnp.sum(e02 + e1, axis=-1, keepdims=True)
    p02 = e02 * il
    p1 = e1 * il
    g02 = jnp.where(low, gp[:, 2 * n:], gp[:, :n])
    g1 = gp[:, n:2 * n]
    rd = jnp.sum(p02 * g02 + p1 * g1, axis=-1, keepdims=True)
    d02 = p02 * (g02 - rd) * SCALE
    d1 = p1 * (g1 - rd) * SCALE

    def spread(a02, a1):
        return jnp.concatenate(
            [jnp.where(low, 0.0, a02).astype(BF16), a1.astype(BF16), jnp.where(low, a02, 0.0).astype(BF16)],
            axis=1,
        )

    plow = spread(p02, p1)
    gs = spread(d02, d1)
    out = dot(plow, v, 1, 0)
    dq = dot(gs, kn, 1, 0)
    dk = dot(gs, qn, 0, 0)
    dv = dot(plow, c, 0, 0)
    gq = norm_back(dq, unit, inv, q_gain)
    return out.astype(BF16), gq.astype(BF16), dk, dv, jnp.sum(dq * unit, axis=0, keepdims=True)


def kernel(
    n_seq, n_dp, heads,
    q_hbm, k_hbm, v_hbm, seg_hbm, d_hbm, qg_ref, kg_ref,
    o_hbm, gq_hbm, gk_hbm, gv_hbm, gain_ref,
    qbuf, dbuf, kbuf, vbuf, sbuf, bias, gtx, grx, own, obuf, qgbuf, fbuf, gall, gdp,
    loc_sem, ps_sem, pr_sem, hs_sem, hr_sem, sls, sps, spr, shs, shr,
    gs_sem, gr_sem, ol_sem, os_sem, or_sem, as_sem, ar_sem, ds_sem, dr_sem,
):
    me = lax.axis_index("seq")
    my_dp = lax.axis_index("dp")
    core = lax.rem(me, 2)
    other = 1 - core
    partner = me + 1 - 2 * core
    first = me - core
    has_prev = first >= 2
    has_next = first + 2 < n_seq
    tok = HD

    def cols(half, h, width):
        return pl.ds(pl.multiple_of((half * heads + h) * width, width), width)

    def rows(block):
        return pl.ds(pl.multiple_of(block * tok, tok), tok)

    def remote(src, dst, ss, rs, dev):
        return pltpu.make_async_remote_copy(
            src_ref=src, dst_ref=dst, send_sem=ss, recv_sem=rs,
            device_id={"seq": dev}, device_id_type=pl.DeviceIdType.MESH,
        )

    ins = (q_hbm, k_hbm, v_hbm, d_hbm)
    widths = (2 * HD, HD, HD, 2 * HD)

    def in_dst(kind, h, block):
        if kind == 0:
            return qbuf.at[h, block]
        if kind == 3:
            return dbuf.at[h, block]
        return (kbuf if kind == 1 else vbuf).at[h, rows(2 + block)]

    def local_in(kind, h):
        return pltpu.make_async_copy(
            ins[kind].at[0, :, cols(core, h, widths[kind])], in_dst(kind, h, core), loc_sem.at[kind, h])

    def partner_in(kind, h):
        return remote(
            ins[kind].at[0, :, cols(other, h, widths[kind])], in_dst(kind, h, core),
            ps_sem.at[kind, h], pr_sem.at[kind, h], partner)

    def partner_in_recv(kind, h):
        return remote(
            ins[kind].at[0, :, cols(core, h, widths[kind])], in_dst(kind, h, other),
            ps_sem.at[kind, h], pr_sem.at[kind, h], partner)

    def halo_send(t, kv, h):
        return remote(
            ins[1 + kv].at[0, :, cols(t, h, HD)], (kbuf, vbuf)[kv].at[h, rows(core)],
            hs_sem.at[t, kv, h], hr_sem.at[core, kv, h], first + 2 + t)

    def halo_recv(s, kv, h):
        return remote(
            ins[1 + kv].at[0, :, cols(core, h, HD)], (kbuf, vbuf)[kv].at[h, pl.ds(s * tok, tok)],
            hs_sem.at[s, kv, h], hr_sem.at[s, kv, h], partner)

    def seg_send(t):
        return remote(seg_hbm, sbuf.at[core], shs.at[t], shr.at[core], first + 2 + t)

    def seg_recv(s):
        return remote(seg_hbm, sbuf.at[s], shs.at[s], shr.at[s], partner)

    seg_local = pltpu.make_async_copy(seg_hbm, sbuf.at[2 + core], sls.at[0])
    seg_partner = remote(seg_hbm, sbuf.at[2 + core], sps.at[0], spr.at[0], partner)
    seg_partner_recv = remote(seg_hbm, sbuf.at[2 + other], sps.at[0], spr.at[0], partner)

    barrier = pltpu.get_barrier_semaphore()

    def greet(k, carry):
        pl.semaphore_signal(barrier, inc=1, device_id={"seq": lax.rem(me + k, n_seq)},
                            device_id_type=pl.DeviceIdType.MESH)
        return carry

    def greet_dp(k, carry):
        pl.semaphore_signal(barrier, inc=1, device_id={"dp": lax.rem(my_dp + k, n_dp)},
                            device_id_type=pl.DeviceIdType.MESH)
        return carry

    lax.fori_loop(1, n_seq, greet, 0)
    lax.fori_loop(1, n_dp, greet_dp, 0)

    seg_local.start()
    for h in range(heads):
        for kind in range(4):
            local_in(kind, h).start()

    @pl.when(jnp.logical_not(has_prev))
    def _():
        for h in range(heads):
            kbuf[h, pl.ds(0, 2 * tok)] = jnp.zeros((2 * tok, HD), BF16)
            vbuf[h, pl.ds(0, 2 * tok)] = jnp.zeros((2 * tok, HD), BF16)
        sbuf[0] = jnp.full((1, tok), -1, jnp.int32)
        sbuf[1] = jnp.full((1, tok), -1, jnp.int32)

    @pl.when(jnp.logical_not(has_next))
    def _():
        for h in range(heads):
            for kv in range(2):
                grx[h, kv] = jnp.zeros((2 * tok, HD), F32)

    pl.semaphore_wait(barrier, n_seq - 1 + n_dp - 1)

    seg_partner.start()

    @pl.when(has_next)
    def _():
        for t in range(2):
            seg_send(t).start()

    for h in range(heads):
        @pl.when(has_next)
        def _():
            for t in range(2):
                for kv in range(2):
                    halo_send(t, kv, h).start()
        for kind in range(4):
            partner_in(kind, h).start()

    seg_local.wait()
    seg_partner_recv.wait_recv()

    @pl.when(has_prev)
    def _():
        for s in range(2):
            seg_recv(s).wait_recv()

    row_i = lax.broadcasted_iota(jnp.int32, (tok, tok), 0)
    col_i = lax.broadcasted_iota(jnp.int32, (tok, tok), 1)
    lower = col_i <= row_i
    docs = [jnp.broadcast_to(sbuf[i], (tok, tok)) for i in range(4)]
    for blk in range(2):
        mine = jnp.transpose(docs[blk + 2])
        b02 = jnp.where(mine == jnp.where(lower, docs[blk + 2], docs[blk]), 0.0, -1e30)
        b1 = jnp.where(mine == docs[blk + 1], 0.0, -1e30)
        for half in range(2):
            bias[blk, 0, pl.ds(half * tok, tok)] = b02
            bias[blk, 1, pl.ds(half * tok, tok)] = b1

    q_gain = qg_ref[...]
    k_gain = kg_ref[...]

    outs = (o_hbm, gq_hbm, gk_hbm, gv_hbm)

    def out_src(kind, h, block):
        if kind == 0:
            return obuf.at[h, block]
        if kind == 1:
            return qgbuf.at[h, block]
        return fbuf.at[h, kind - 2, block]

    out_widths = (2 * HD, 2 * HD, HD, HD)

    def local_out(kind, h):
        return pltpu.make_async_copy(
            out_src(kind, h, core), outs[kind].at[0, :, cols(core, h, out_widths[kind])], ol_sem.at[kind, h])

    def partner_out(kind, h):
        return remote(
            out_src(kind, h, other), outs[kind].at[0, :, cols(core, h, out_widths[kind])],
            os_sem.at[kind, h], or_sem.at[kind, h], partner)

    def partner_out_recv(kind, h):
        return remote(
            out_src(kind, h, other), outs[kind].at[0, :, cols(other, h, out_widths[kind])],
            os_sem.at[kind, h], or_sem.at[kind, h], partner)

    def grad_send(h):
        return remote(gtx.at[h], grx.at[h], gs_sem.at[h], gr_sem.at[h], me - 2)

    def head_step(h, q_term):
        for kind in range(4):
            local_in(kind, h).wait()
            partner_in_recv(kind, h).wait_recv()

        @pl.when(has_prev)
        def _():
            for s in range(2):
                for kv in range(2):
                    halo_recv(s, kv, h).wait_recv()

        low = (lax.broadcasted_iota(jnp.int32, (2 * tok, tok), 1)
               <= lax.rem(lax.broadcasted_iota(jnp.int32, (2 * tok, tok), 0), tok))
        kx = kbuf[h].astype(F32)
        kn = (kx * inv_rms(kx) * k_gain).astype(BF16)
        vv = vbuf[h]
        dks, dvs = [], []
        for blk in range(2):
            ks = slice(blk * tok, blk * tok + 3 * tok)
            out, gq, dk, dv, term = unit_step(
                qbuf[h, blk], dbuf[h, blk], kn[ks], vv[ks], bias[blk, 0], bias[blk, 1], low, q_gain)
            q_term = q_term + term
            obuf[h, blk, :, :HD] = out[:tok]
            obuf[h, blk, :, HD:] = out[tok:]
            qgbuf[h, blk, :, :HD] = gq[:tok]
            qgbuf[h, blk, :, HD:] = gq[tok:]
            dks.append(dk)
            dvs.append(dv)
        for kv, (a, b) in enumerate((dks, dvs)):
            gtx[h, kv, pl.ds(0, tok)] = a[:tok]
            gtx[h, kv, pl.ds(tok, tok)] = a[tok:2 * tok] + b[:tok]
            own[h, kv, pl.ds(0, tok)] = a[2 * tok:] + b[tok:2 * tok]
            own[h, kv, pl.ds(tok, tok)] = b[2 * tok:]

        @pl.when(has_prev)
        def _():
            grad_send(h).start()

        for kind in range(2):
            local_out(kind, h).start()
            partner_out(kind, h).start()
        return q_term

    q_term = lax.fori_loop(0, heads, head_step, jnp.zeros((1, HD), F32))

    def final_step(h, k_term):
        @pl.when(has_next)
        def _():
            grad_send(h).wait_recv()
        gk = own[h, 0] + grx[h, 0]
        gv = own[h, 1] + grx[h, 1]
        kx = kbuf[h, pl.ds(2 * tok, 2 * tok)].astype(F32)
        inv = inv_rms(kx)
        unit = kx * inv
        gkb = norm_back(gk, unit, inv, k_gain).astype(BF16)
        gvb = gv.astype(BF16)
        for blk in range(2):
            fbuf[h, 0, blk] = gkb[blk * tok:(blk + 1) * tok]
            fbuf[h, 1, blk] = gvb[blk * tok:(blk + 1) * tok]
        for kind in (2, 3):
            partner_out(kind, h).start()
            local_out(kind, h).start()
        return k_term + jnp.sum(gk * unit, axis=0, keepdims=True)

    k_term = lax.fori_loop(0, heads, final_step, jnp.zeros((1, HD), F32))

    gall[me] = jnp.concatenate([q_term, k_term], axis=0)

    def seq_copy(k, peer):
        return remote(gall.at[peer], gall.at[peer], as_sem.at[k], ar_sem.at[k], lax.rem(me + k, n_seq))

    def seq_go(k, carry):
        seq_copy(k, me).start()
        return carry

    def seq_wait(k, carry):
        seq_copy(k, lax.rem(me - k + n_seq, n_seq)).wait_recv()
        return carry

    def seq_done(k, carry):
        seq_copy(k, me).wait_send()
        return carry

    lax.fori_loop(1, n_seq, seq_go, 0)
    lax.fori_loop(1, n_seq, seq_wait, 0)
    gdp[my_dp] = jnp.sum(gall[...], axis=0)

    def dp_copy(k, slot):
        return pltpu.make_async_remote_copy(
            src_ref=gdp.at[slot], dst_ref=gdp.at[slot], send_sem=ds_sem.at[k], recv_sem=dr_sem.at[k],
            device_id={"dp": lax.rem(my_dp + k, n_dp)}, device_id_type=pl.DeviceIdType.MESH)

    def dp_go(k, carry):
        dp_copy(k, my_dp).start()
        return carry

    def dp_wait(k, carry):
        dp_copy(k, lax.rem(my_dp - k + n_dp, n_dp)).wait_recv()
        return carry

    def dp_done(k, carry):
        dp_copy(k, my_dp).wait_send()
        return carry

    lax.fori_loop(1, n_dp, dp_go, 0)

    def drain(h, carry):
        for kind in range(4):
            partner_in(kind, h).wait_send()
            local_out(kind, h).wait()
            partner_out(kind, h).wait_send()
            partner_out_recv(kind, h).wait_recv()

        @pl.when(has_next)
        def _():
            for t in range(2):
                for kv in range(2):
                    halo_send(t, kv, h).wait_send()

        @pl.when(has_prev)
        def _():
            grad_send(h).wait_send()
        return carry

    lax.fori_loop(0, heads, drain, 0)
    seg_partner.wait_send()

    @pl.when(has_next)
    def _():
        for t in range(2):
            seg_send(t).wait_send()

    lax.fori_loop(1, n_seq, seq_done, 0)
    lax.fori_loop(1, n_dp, dp_wait, 0)
    gain_ref[...] = jnp.sum(gdp[...], axis=0) * (n_seq * n_dp * tok) ** (-0.5)
    lax.fori_loop(1, n_dp, dp_done, 0)


def per_device(n_seq, n_dp, queries, keys, values, segments, q_gain, k_gain, d_attn):
    tok = queries.shape[1]
    assert tok == HD and WINDOW == 2 * tok
    heads = keys.shape[2] // HD // 2
    any_spec = pl.BlockSpec(memory_space=pl.ANY)
    vmem = pl.BlockSpec(memory_space=pltpu.VMEM)
    dma = pltpu.SemaphoreType.DMA
    shape = jax.ShapeDtypeStruct
    return pl.pallas_call(
        functools.partial(kernel, n_seq, n_dp, heads),
        out_shape=(
            shape(queries.shape, BF16), shape(queries.shape, BF16),
            shape(keys.shape, BF16), shape(keys.shape, BF16), shape((2, HD), F32),
        ),
        in_specs=[any_spec] * 5 + [vmem] * 2,
        out_specs=(any_spec,) * 4 + (vmem,),
        scratch_shapes=[
            pltpu.VMEM((heads, 2, tok, 2 * HD), BF16),
            pltpu.VMEM((heads, 2, tok, 2 * HD), BF16),
            pltpu.VMEM((heads, 4 * tok, HD), BF16),
            pltpu.VMEM((heads, 4 * tok, HD), BF16),
            pltpu.VMEM((4, 1, tok), jnp.int32),
            pltpu.VMEM((2, 2, 2 * tok, tok), F32),
            pltpu.VMEM((heads, 2, 2 * tok, HD), F32),
            pltpu.VMEM((heads, 2, 2 * tok, HD), F32),
            pltpu.VMEM((heads, 2, 2 * tok, HD), F32),
            pltpu.VMEM((heads, 2, tok, 2 * HD), BF16),
            pltpu.VMEM((heads, 2, tok, 2 * HD), BF16),
            pltpu.VMEM((heads, 2, 2, tok, HD), BF16),
            pltpu.VMEM((n_seq, 2, HD), F32),
            pltpu.VMEM((n_dp, 2, HD), F32),
            dma((4, heads)), dma((4, heads)), dma((4, heads)),
            dma((2, 2, heads)), dma((2, 2, heads)),
            dma((1,)), dma((1,)), dma((1,)), dma((2,)), dma((2,)),
            dma((heads,)), dma((heads,)),
            dma((4, heads)), dma((4, heads)), dma((4, heads)),
            dma((n_seq,)), dma((n_seq,)), dma((n_dp,)), dma((n_dp,)),
        ],
        compiler_params=pltpu.CompilerParams(
            collective_id=0, has_side_effects=True, vmem_limit_bytes=40 << 20),
    )(queries, keys, values, segments, d_attn, q_gain.reshape(1, HD), k_gain.reshape(1, HD))


def solution(mesh):
    tokens = P("dp", "seq", None)
    return jax.shard_map(
        functools.partial(per_device, mesh.shape["seq"], mesh.shape["dp"]),
        mesh=mesh,
        in_specs=(tokens, tokens, tokens, P("dp", "seq"), P(), P(), tokens),
        out_specs=(tokens, tokens, tokens, tokens, P()),
        check_vma=False,
    )
```

```python
import functools
import math

import jax
import jax.numpy as jnp
from jax import lax
from jax.experimental import pallas as pl
from jax.experimental.pallas import tpu as pltpu
from jax.sharding import PartitionSpec as P

QPA = 168
WINDOW = 256
HD = 128
EPS = 1e-06
SCALE = QPA ** (-0.5)
EXP2_SCALE = SCALE * math.log2(math.e)
F32 = jnp.float32
BF16 = jnp.bfloat16


def dot(a, b, ca, cb):
    return lax.dot_general(a, b, (((ca,), (cb,)), ((), ())), preferred_element_type=F32)


def inv_rms(x):
    return 1.0 / jnp.sqrt(jnp.mean(x * x, axis=-1, keepdims=True) + EPS)


def stack_heads(x):
    return jnp.concatenate([x[:, :HD], x[:, HD:]], axis=0)


def norm_back(grad, unit, inv, gain):
    t = grad * gain
    return (t - unit * jnp.mean(t * unit, axis=-1, keepdims=True)) * inv


def unit_step(q_raw, c_raw, kn, v, bias02, bias1, low, q_gain):
    x = stack_heads(q_raw).astype(F32)
    c = stack_heads(c_raw)
    inv = inv_rms(x)
    unit = x * inv
    qn = (unit * q_gain).astype(BF16)
    s = dot(qn, kn, 1, 1)
    gp = dot(c, v, 1, 1)
    n = HD
    x02 = jnp.where(low, s[:, 2 * n:], s[:, :n]) + bias02
    x1 = s[:, n:2 * n] + bias1
    m = jnp.max(jnp.maximum(x02, x1), axis=-1, keepdims=True)
    e02 = jnp.exp2((x02 - m) * EXP2_SCALE)
    e1 = jnp.exp2((x1 - m) * EXP2_SCALE)
    il = 1.0 / jnp.sum(e02 + e1, axis=-1, keepdims=True)
    p02 = e02 * il
    p1 = e1 * il
    g02 = jnp.where(low, gp[:, 2 * n:], gp[:, :n])
    g1 = gp[:, n:2 * n]
    rd = jnp.sum(p02 * g02 + p1 * g1, axis=-1, keepdims=True)
    d02 = p02 * (g02 - rd) * SCALE
    d1 = p1 * (g1 - rd) * SCALE

    def spread(a02, a1):
        return jnp.concatenate(
            [jnp.where(low, 0.0, a02).astype(BF16), a1.astype(BF16), jnp.where(low, a02, 0.0).astype(BF16)],
            axis=1,
        )

    plow = spread(p02, p1)
    gs = spread(d02, d1)
    out = dot(plow, v, 1, 0)
    dq = dot(gs, kn, 1, 0)
    dk = dot(gs, qn, 0, 0)
    dv = dot(plow, c, 0, 0)
    gq = norm_back(dq, unit, inv, q_gain)
    return out.astype(BF16), gq.astype(BF16), dk, dv, jnp.sum(dq * unit, axis=0, keepdims=True)


def kernel(
    n_seq, n_dp, heads,
    q_hbm, k_hbm, v_hbm, seg_hbm, d_hbm, qg_ref, kg_ref,
    o_hbm, gq_hbm, gk_hbm, gv_hbm, gain_ref,
    qbuf, dbuf, kbuf, vbuf, sbuf, bias, gtx, grx, own, obuf, qgbuf, fbuf, gall, gdp,
    loc_sem, ps_sem, pr_sem, hs_sem, hr_sem, sls, sps, spr, shs, shr,
    gs_sem, gr_sem, ol_sem, os_sem, or_sem, as_sem, ar_sem,
):
    me = lax.axis_index("seq")
    my_dp = lax.axis_index("dp")
    core = lax.rem(me, 2)
    other = 1 - core
    partner = me + 1 - 2 * core
    first = me - core
    has_prev = first >= 2
    has_next = first + 2 < n_seq
    tok = HD

    def cols(half, h, width):
        return pl.ds(pl.multiple_of((half * heads + h) * width, width), width)

    def rows(block):
        return pl.ds(pl.multiple_of(block * tok, tok), tok)

    def remote(src, dst, ss, rs, dev):
        return pltpu.make_async_remote_copy(
            src_ref=src, dst_ref=dst, send_sem=ss, recv_sem=rs,
            device_id={"seq": dev}, device_id_type=pl.DeviceIdType.MESH,
        )

    ins = (q_hbm, k_hbm, v_hbm, d_hbm)
    widths = (2 * HD, HD, HD, 2 * HD)

    def in_dst(kind, h, block):
        if kind == 0:
            return qbuf.at[h, block]
        if kind == 3:
            return dbuf.at[h, block]
        return (kbuf if kind == 1 else vbuf).at[h, rows(2 + block)]

    def local_in(kind, h):
        return pltpu.make_async_copy(
            ins[kind].at[0, :, cols(core, h, widths[kind])], in_dst(kind, h, core), loc_sem.at[kind, h])

    def partner_in(kind, h):
        return remote(
            ins[kind].at[0, :, cols(other, h, widths[kind])], in_dst(kind, h, core),
            ps_sem.at[kind, h], pr_sem.at[kind, h], partner)

    def partner_in_recv(kind, h):
        return remote(
            ins[kind].at[0, :, cols(core, h, widths[kind])], in_dst(kind, h, other),
            ps_sem.at[kind, h], pr_sem.at[kind, h], partner)

    def halo_send(t, kv, h):
        return remote(
            ins[1 + kv].at[0, :, cols(t, h, HD)], (kbuf, vbuf)[kv].at[h, rows(core)],
            hs_sem.at[t, kv, h], hr_sem.at[core, kv, h], first + 2 + t)

    def halo_recv(s, kv, h):
        return remote(
            ins[1 + kv].at[0, :, cols(core, h, HD)], (kbuf, vbuf)[kv].at[h, pl.ds(s * tok, tok)],
            hs_sem.at[s, kv, h], hr_sem.at[s, kv, h], partner)

    def seg_send(t):
        return remote(seg_hbm, sbuf.at[core], shs.at[t], shr.at[core], first + 2 + t)

    def seg_recv(s):
        return remote(seg_hbm, sbuf.at[s], shs.at[s], shr.at[s], partner)

    seg_local = pltpu.make_async_copy(seg_hbm, sbuf.at[2 + core], sls.at[0])
    seg_partner = remote(seg_hbm, sbuf.at[2 + core], sps.at[0], spr.at[0], partner)
    seg_partner_recv = remote(seg_hbm, sbuf.at[2 + other], sps.at[0], spr.at[0], partner)

    barrier = pltpu.get_barrier_semaphore()

    def greet(axis, dev):
        pl.semaphore_signal(barrier, inc=1, device_id={axis: dev}, device_id_type=pl.DeviceIdType.MESH)

    def flip(index, bit):
        return index + bit - 2 * bit * lax.rem(index // bit, 2)

    seq_bits = [1 << i for i in range(n_seq.bit_length() - 1)]
    dp_bits = [1 << i for i in range(n_dp.bit_length() - 1)]
    hops = [("seq", b, me) for b in seq_bits] + [("dp", b, my_dp) for b in dp_bits]

    greet("seq", partner)

    @pl.when(has_next)
    def _():
        greet("seq", first + 2)
        greet("seq", first + 3)

    @pl.when(has_prev)
    def _():
        greet("seq", first - 2)
        greet("seq", first - 1)

    for axis, bit, index in hops[2:]:
        greet(axis, flip(index, bit))

    seg_local.start()
    for h in range(heads):
        for kind in range(4):
            local_in(kind, h).start()

    @pl.when(jnp.logical_not(has_prev))
    def _():
        for h in range(heads):
            kbuf[h, pl.ds(0, 2 * tok)] = jnp.zeros((2 * tok, HD), BF16)
            vbuf[h, pl.ds(0, 2 * tok)] = jnp.zeros((2 * tok, HD), BF16)
        sbuf[0] = jnp.full((1, tok), -1, jnp.int32)
        sbuf[1] = jnp.full((1, tok), -1, jnp.int32)

    @pl.when(jnp.logical_not(has_next))
    def _():
        for h in range(heads):
            for kv in range(2):
                grx[h, kv] = jnp.zeros((2 * tok, HD), F32)

    greeted = 1 + len(hops) - 2
    pl.semaphore_wait(barrier, greeted + 2 * has_prev.astype(jnp.int32) + 2 * has_next.astype(jnp.int32))

    seg_partner.start()

    @pl.when(has_next)
    def _():
        for t in range(2):
            seg_send(t).start()

    for h in range(heads):
        @pl.when(has_next)
        def _():
            for t in range(2):
                for kv in range(2):
                    halo_send(t, kv, h).start()
        for kind in range(4):
            partner_in(kind, h).start()

    seg_local.wait()
    seg_partner_recv.wait_recv()

    @pl.when(has_prev)
    def _():
        for s in range(2):
            seg_recv(s).wait_recv()

    row_i = lax.broadcasted_iota(jnp.int32, (tok, tok), 0)
    col_i = lax.broadcasted_iota(jnp.int32, (tok, tok), 1)
    lower = col_i <= row_i
    docs = [jnp.broadcast_to(sbuf[i], (tok, tok)) for i in range(4)]
    for blk in range(2):
        mine = jnp.transpose(docs[blk + 2])
        b02 = jnp.where(mine == jnp.where(lower, docs[blk + 2], docs[blk]), 0.0, -1e30)
        b1 = jnp.where(mine == docs[blk + 1], 0.0, -1e30)
        for half in range(2):
            bias[blk, 0, pl.ds(half * tok, tok)] = b02
            bias[blk, 1, pl.ds(half * tok, tok)] = b1

    q_gain = qg_ref[...]
    k_gain = kg_ref[...]

    outs = (o_hbm, gq_hbm, gk_hbm, gv_hbm)

    def out_src(kind, h, block):
        if kind == 0:
            return obuf.at[h, block]
        if kind == 1:
            return qgbuf.at[h, block]
        return fbuf.at[h, kind - 2, block]

    out_widths = (2 * HD, 2 * HD, HD, HD)

    def local_out(kind, h):
        return pltpu.make_async_copy(
            out_src(kind, h, core), outs[kind].at[0, :, cols(core, h, out_widths[kind])], ol_sem.at[kind, h])

    def partner_out(kind, h):
        return remote(
            out_src(kind, h, other), outs[kind].at[0, :, cols(core, h, out_widths[kind])],
            os_sem.at[kind, h], or_sem.at[kind, h], partner)

    def partner_out_recv(kind, h):
        return remote(
            out_src(kind, h, other), outs[kind].at[0, :, cols(other, h, out_widths[kind])],
            os_sem.at[kind, h], or_sem.at[kind, h], partner)

    def grad_send(h):
        return remote(gtx.at[h], grx.at[h], gs_sem.at[h], gr_sem.at[h], me - 2)

    def head_step(h, terms):
        q_term, k_term = terms
        for kind in range(4):
            local_in(kind, h).wait()
            partner_in_recv(kind, h).wait_recv()

        @pl.when(has_prev)
        def _():
            for s in range(2):
                for kv in range(2):
                    halo_recv(s, kv, h).wait_recv()

        low = (lax.broadcasted_iota(jnp.int32, (2 * tok, tok), 1)
               <= lax.rem(lax.broadcasted_iota(jnp.int32, (2 * tok, tok), 0), tok))
        kx = kbuf[h].astype(F32)
        k_unit = kx * inv_rms(kx)
        kn = (k_unit * k_gain).astype(BF16)
        vv = vbuf[h]
        dks, dvs = [], []
        for blk in range(2):
            ks = slice(blk * tok, blk * tok + 3 * tok)
            out, gq, dk, dv, term = unit_step(
                qbuf[h, blk], dbuf[h, blk], kn[ks], vv[ks], bias[blk, 0], bias[blk, 1], low, q_gain)
            q_term = q_term + term
            obuf[h, blk, :, :HD] = out[:tok]
            obuf[h, blk, :, HD:] = out[tok:]
            qgbuf[h, blk, :, :HD] = gq[:tok]
            qgbuf[h, blk, :, HD:] = gq[tok:]
            dks.append(dk)
            dvs.append(dv)
        for kv, (a, b) in enumerate((dks, dvs)):
            gtx[h, kv, pl.ds(0, tok)] = a[:tok]
            gtx[h, kv, pl.ds(tok, tok)] = a[tok:2 * tok] + b[:tok]
            own[h, kv, pl.ds(0, tok)] = a[2 * tok:] + b[tok:2 * tok]
            own[h, kv, pl.ds(tok, tok)] = b[2 * tok:]

        @pl.when(has_prev)
        def _():
            grad_send(h).start()

        for kind in range(2):
            local_out(kind, h).start()
            partner_out(kind, h).start()
        a, b = dks
        for rows_of, grad in (
            (slice(0, tok), a[:tok]),
            (slice(tok, 2 * tok), a[tok:2 * tok] + b[:tok]),
            (slice(2 * tok, 3 * tok), a[2 * tok:] + b[tok:2 * tok]),
            (slice(3 * tok, 4 * tok), b[2 * tok:]),
        ):
            k_term = k_term + jnp.sum(grad * k_unit[rows_of], axis=0, keepdims=True)
        return q_term, k_term

    zero_row = jnp.zeros((1, HD), F32)
    q_term, k_term = lax.fori_loop(0, heads, head_step, (zero_row, zero_row))

    def final_step(h):
        @pl.when(has_next)
        def _():
            grad_send(h).wait_recv()
        gk = own[h, 0] + grx[h, 0]
        gv = own[h, 1] + grx[h, 1]
        kx = kbuf[h, pl.ds(2 * tok, 2 * tok)].astype(F32)
        inv = inv_rms(kx)
        unit = kx * inv
        gkb = norm_back(gk, unit, inv, k_gain).astype(BF16)
        gvb = gv.astype(BF16)
        for blk in range(2):
            fbuf[h, 0, blk] = gkb[blk * tok:(blk + 1) * tok]
            fbuf[h, 1, blk] = gvb[blk * tok:(blk + 1) * tok]
        for kind in (2, 3):
            partner_out(kind, h).start()
            local_out(kind, h).start()

    def term_copy(i):
        axis, bit, index = hops[i]
        return pltpu.make_async_remote_copy(
            src_ref=gall.at[i], dst_ref=gdp.at[i], send_sem=as_sem.at[i], recv_sem=ar_sem.at[i],
            device_id={axis: flip(index, bit)}, device_id_type=pl.DeviceIdType.MESH)

    gall[0] = jnp.concatenate([q_term, k_term], axis=0)
    term_copy(0).start()
    waits = [i * heads // len(hops) for i in range(len(hops))]
    for h in range(heads):
        final_step(h)
        for i, at in enumerate(waits):
            if at == h:
                term_copy(i).wait_recv()
                gall[i + 1] = gall[i] + gdp[i]
                if i + 1 < len(hops):
                    term_copy(i + 1).start()
    gain_ref[...] = gall[len(hops)] * (n_seq * n_dp * tok) ** (-0.5)

    def drain(h, carry):
        for kind in range(4):
            partner_in(kind, h).wait_send()
            local_out(kind, h).wait()
            partner_out(kind, h).wait_send()
            partner_out_recv(kind, h).wait_recv()

        @pl.when(has_next)
        def _():
            for t in range(2):
                for kv in range(2):
                    halo_send(t, kv, h).wait_send()

        @pl.when(has_prev)
        def _():
            grad_send(h).wait_send()
        return carry

    lax.fori_loop(0, heads, drain, 0)
    seg_partner.wait_send()

    @pl.when(has_next)
    def _():
        for t in range(2):
            seg_send(t).wait_send()

    for i in range(len(hops)):
        term_copy(i).wait_send()


def place(*refs):
    sem = refs[10]
    copies = [pltpu.make_async_copy(refs[i], refs[5 + i], sem.at[i]) for i in range(5)]
    for copy in copies:
        copy.start()
    for copy in copies:
        copy.wait()


def per_device(n_seq, n_dp, queries, keys, values, segments, q_gain, k_gain, d_attn):
    tok = queries.shape[1]
    assert tok == HD and WINDOW == 2 * tok
    heads = keys.shape[2] // HD // 2
    n_hops = n_seq.bit_length() + n_dp.bit_length() - 2
    assert n_seq & (n_seq - 1) == 0 and n_dp & (n_dp - 1) == 0 and n_seq >= 4
    any_spec = pl.BlockSpec(memory_space=pl.ANY)
    vmem = pl.BlockSpec(memory_space=pltpu.VMEM)
    dma = pltpu.SemaphoreType.DMA
    shape = jax.ShapeDtypeStruct
    queries, keys, values, segments, d_attn = (
        pltpu.with_memory_space_constraint(x, pltpu.HBM) for x in (queries, keys, values, segments, d_attn))
    results = pl.pallas_call(
        functools.partial(kernel, n_seq, n_dp, heads),
        out_shape=(
            shape(queries.shape, BF16), shape(queries.shape, BF16),
            shape(keys.shape, BF16), shape(keys.shape, BF16), shape((2, HD), F32),
        ),
        in_specs=[pl.BlockSpec(memory_space=pltpu.HBM)] * 5 + [vmem] * 2,
        out_specs=(any_spec,) * 4 + (vmem,),
        scratch_shapes=[
            pltpu.VMEM((heads, 2, tok, 2 * HD), BF16),
            pltpu.VMEM((heads, 2, tok, 2 * HD), BF16),
            pltpu.VMEM((heads, 4 * tok, HD), BF16),
            pltpu.VMEM((heads, 4 * tok, HD), BF16),
            pltpu.VMEM((4, 1, tok), jnp.int32),
            pltpu.VMEM((2, 2, 2 * tok, tok), F32),
            pltpu.VMEM((heads, 2, 2 * tok, HD), F32),
            pltpu.VMEM((heads, 2, 2 * tok, HD), F32),
            pltpu.VMEM((heads, 2, 2 * tok, HD), F32),
            pltpu.VMEM((heads, 2, tok, 2 * HD), BF16),
            pltpu.VMEM((heads, 2, tok, 2 * HD), BF16),
            pltpu.VMEM((heads, 2, 2, tok, HD), BF16),
            pltpu.VMEM((n_hops + 1, 2, HD), F32),
            pltpu.VMEM((n_hops, 2, HD), F32),
            dma((4, heads)), dma((4, heads)), dma((4, heads)),
            dma((2, 2, heads)), dma((2, 2, heads)),
            dma((1,)), dma((1,)), dma((1,)), dma((2,)), dma((2,)),
            dma((heads,)), dma((heads,)),
            dma((4, heads)), dma((4, heads)), dma((4, heads)),
            dma((n_hops,)), dma((n_hops,)),
        ],
        compiler_params=pltpu.CompilerParams(
            collective_id=0, has_side_effects=True, vmem_limit_bytes=40 << 20),
    )(queries, keys, values, segments, d_attn, q_gain.reshape(1, HD), k_gain.reshape(1, HD))
    return pl.pallas_call(
        place,
        out_shape=tuple(shape(x.shape, x.dtype) for x in results),
        in_specs=[vmem] * 5,
        out_specs=(any_spec,) * 5,
        scratch_shapes=[dma((5,))],
        compiler_params=pltpu.CompilerParams(vmem_limit_bytes=50 << 20),
    )(*results)


def solution(mesh):
    tokens = P("dp", "seq", None)
    return jax.shard_map(
        functools.partial(per_device, mesh.shape["seq"], mesh.shape["dp"]),
        mesh=mesh,
        in_specs=(tokens, tokens, tokens, P("dp", "seq"), P(), P(), tokens),
        out_specs=(tokens, tokens, tokens, tokens, P()),
        check_vma=False,
    )
```

```python
import functools
import math

import jax
import jax.numpy as jnp
from jax import lax
from jax.experimental import pallas as pl
from jax.experimental.pallas import tpu as pltpu
from jax.sharding import PartitionSpec as P

QPA = 168
WINDOW = 256
HD = 128
EPS = 1e-06
SCALE = QPA ** (-0.5)
EXP2_SCALE = SCALE * math.log2(math.e)
CODE = 32767.0
F32 = jnp.float32
BF16 = jnp.bfloat16


def dot(a, b, ca, cb):
    return lax.dot_general(a, b, (((ca,), (cb,)), ((), ())), preferred_element_type=F32)


def inv_rms(x):
    return 1.0 / jnp.sqrt(jnp.mean(x * x, axis=-1, keepdims=True) + EPS)


def stack_heads(x):
    return jnp.concatenate([x[:, :HD], x[:, HD:]], axis=0)


def norm_back(grad, unit, inv, gain):
    t = grad * gain
    return (t - unit * jnp.mean(t * unit, axis=-1, keepdims=True)) * inv


def unit_step(q_raw, c_raw, kn, v, bias02, bias1, low, q_gain):
    x = stack_heads(q_raw).astype(F32)
    c = stack_heads(c_raw)
    inv = inv_rms(x)
    unit = x * inv
    qn = (unit * q_gain).astype(BF16)
    s = dot(qn, kn, 1, 1)
    gp = dot(c, v, 1, 1)
    n = HD
    x02 = jnp.where(low, s[:, 2 * n:], s[:, :n]) + bias02
    x1 = s[:, n:2 * n] + bias1
    m = jnp.max(jnp.maximum(x02, x1), axis=-1, keepdims=True)
    e02 = jnp.exp2((x02 - m) * EXP2_SCALE)
    e1 = jnp.exp2((x1 - m) * EXP2_SCALE)
    il = 1.0 / jnp.sum(e02 + e1, axis=-1, keepdims=True)
    p02 = e02 * il
    p1 = e1 * il
    g02 = jnp.where(low, gp[:, 2 * n:], gp[:, :n])
    g1 = gp[:, n:2 * n]
    rd = jnp.sum(p02 * g02 + p1 * g1, axis=-1, keepdims=True)
    d02 = p02 * (g02 - rd) * SCALE
    d1 = p1 * (g1 - rd) * SCALE

    def spread(a02, a1):
        return jnp.concatenate(
            [jnp.where(low, 0.0, a02).astype(BF16), a1.astype(BF16), jnp.where(low, a02, 0.0).astype(BF16)],
            axis=1,
        )

    plow = spread(p02, p1)
    gs = spread(d02, d1)
    out = dot(plow, v, 1, 0)
    dq = dot(gs, kn, 1, 0)
    dk = dot(gs, qn, 0, 0)
    dv = dot(plow, c, 0, 0)
    gq = norm_back(dq, unit, inv, q_gain)
    return out.astype(BF16), gq.astype(BF16), dk, dv, jnp.sum(dq * unit, axis=0, keepdims=True)


def kernel(
    n_seq, n_dp, heads,
    q_hbm, k_hbm, v_hbm, seg_hbm, d_hbm, qg_ref, kg_ref,
    o_hbm, gq_hbm, gk_hbm, gv_hbm, gain_ref,
    qbuf, dbuf, kbuf, vbuf, sbuf, bias, gtx, grx, stx, srx, own, obuf, qgbuf, fbuf, gall, gdp,
    loc_sem, ps_sem, pr_sem, hs_sem, hr_sem, sls, sps, spr, shs, shr,
    gs_sem, gr_sem, ss_sem, sr_sem, ol_sem, os_sem, or_sem, as_sem, ar_sem,
):
    me = lax.axis_index("seq")
    my_dp = lax.axis_index("dp")
    core = lax.rem(me, 2)
    other = 1 - core
    partner = me + 1 - 2 * core
    first = me - core
    has_prev = first >= 2
    has_next = first + 2 < n_seq
    tok = HD

    def cols(half, h, width):
        return pl.ds(pl.multiple_of((half * heads + h) * width, width), width)

    def rows(block):
        return pl.ds(pl.multiple_of(block * tok, tok), tok)

    def remote(src, dst, ss, rs, dev):
        return pltpu.make_async_remote_copy(
            src_ref=src, dst_ref=dst, send_sem=ss, recv_sem=rs,
            device_id={"seq": dev}, device_id_type=pl.DeviceIdType.MESH,
        )

    ins = (q_hbm, k_hbm, v_hbm, d_hbm)
    widths = (2 * HD, HD, HD, 2 * HD)

    def in_dst(kind, h, block):
        if kind == 0:
            return qbuf.at[h, block]
        if kind == 3:
            return dbuf.at[h, block]
        return (kbuf if kind == 1 else vbuf).at[h, rows(2 + block)]

    def local_in(kind, h):
        return pltpu.make_async_copy(
            ins[kind].at[0, :, cols(core, h, widths[kind])], in_dst(kind, h, core), loc_sem.at[kind, h])

    def partner_in(kind, h):
        return remote(
            ins[kind].at[0, :, cols(other, h, widths[kind])], in_dst(kind, h, core),
            ps_sem.at[kind, h], pr_sem.at[kind, h], partner)

    def partner_in_recv(kind, h):
        return remote(
            ins[kind].at[0, :, cols(core, h, widths[kind])], in_dst(kind, h, other),
            ps_sem.at[kind, h], pr_sem.at[kind, h], partner)

    def halo_send(t, kv, h):
        return remote(
            ins[1 + kv].at[0, :, cols(t, h, HD)], (kbuf, vbuf)[kv].at[h, rows(core)],
            hs_sem.at[t, kv, h], hr_sem.at[core, kv, h], first + 2 + t)

    def halo_recv(s, kv, h):
        return remote(
            ins[1 + kv].at[0, :, cols(core, h, HD)], (kbuf, vbuf)[kv].at[h, pl.ds(s * tok, tok)],
            hs_sem.at[s, kv, h], hr_sem.at[s, kv, h], partner)

    def seg_send(t):
        return remote(seg_hbm, sbuf.at[core], shs.at[t], shr.at[core], first + 2 + t)

    def seg_recv(s):
        return remote(seg_hbm, sbuf.at[s], shs.at[s], shr.at[s], partner)

    seg_local = pltpu.make_async_copy(seg_hbm, sbuf.at[2 + core], sls.at[0])
    seg_partner = remote(seg_hbm, sbuf.at[2 + core], sps.at[0], spr.at[0], partner)
    seg_partner_recv = remote(seg_hbm, sbuf.at[2 + other], sps.at[0], spr.at[0], partner)

    barrier = pltpu.get_barrier_semaphore()

    def greet(axis, dev):
        pl.semaphore_signal(barrier, inc=1, device_id={axis: dev}, device_id_type=pl.DeviceIdType.MESH)

    def flip(index, bit):
        return index + bit - 2 * bit * lax.rem(index // bit, 2)

    seq_bits = [1 << i for i in range(n_seq.bit_length() - 1)]
    dp_bits = [1 << i for i in range(n_dp.bit_length() - 1)]
    hops = [("seq", b, me) for b in seq_bits] + [("dp", b, my_dp) for b in dp_bits]

    greet("seq", partner)

    @pl.when(has_next)
    def _():
        greet("seq", first + 2)
        greet("seq", first + 3)

    @pl.when(has_prev)
    def _():
        greet("seq", first - 2)
        greet("seq", first - 1)

    for axis, bit, index in hops[2:]:
        greet(axis, flip(index, bit))

    seg_local.start()
    for h in range(heads):
        for kind in range(4):
            local_in(kind, h).start()

    @pl.when(jnp.logical_not(has_prev))
    def _():
        for h in range(heads):
            kbuf[h, pl.ds(0, 2 * tok)] = jnp.zeros((2 * tok, HD), BF16)
            vbuf[h, pl.ds(0, 2 * tok)] = jnp.zeros((2 * tok, HD), BF16)
        sbuf[0] = jnp.full((1, tok), -1, jnp.int32)
        sbuf[1] = jnp.full((1, tok), -1, jnp.int32)

    @pl.when(jnp.logical_not(has_next))
    def _():
        for h in range(heads):
            for kv in range(2):
                grx[h, kv] = jnp.zeros((2 * tok, HD), jnp.int16)
            srx[h] = jnp.zeros((4, tok), F32)

    greeted = 1 + len(hops) - 2
    pl.semaphore_wait(barrier, greeted + 2 * has_prev.astype(jnp.int32) + 2 * has_next.astype(jnp.int32))

    seg_partner.start()

    @pl.when(has_next)
    def _():
        for t in range(2):
            seg_send(t).start()

    for h in range(heads):
        @pl.when(has_next)
        def _():
            for t in range(2):
                for kv in range(2):
                    halo_send(t, kv, h).start()
        for kind in range(4):
            partner_in(kind, h).start()

    seg_local.wait()
    seg_partner_recv.wait_recv()

    @pl.when(has_prev)
    def _():
        for s in range(2):
            seg_recv(s).wait_recv()

    row_i = lax.broadcasted_iota(jnp.int32, (tok, tok), 0)
    col_i = lax.broadcasted_iota(jnp.int32, (tok, tok), 1)
    lower = col_i <= row_i
    docs = [jnp.broadcast_to(sbuf[i], (tok, tok)) for i in range(4)]
    for blk in range(2):
        mine = jnp.transpose(docs[blk + 2])
        b02 = jnp.where(mine == jnp.where(lower, docs[blk + 2], docs[blk]), 0.0, -1e30)
        b1 = jnp.where(mine == docs[blk + 1], 0.0, -1e30)
        for half in range(2):
            bias[blk, 0, pl.ds(half * tok, tok)] = b02
            bias[blk, 1, pl.ds(half * tok, tok)] = b1

    q_gain = qg_ref[...]
    k_gain = kg_ref[...]

    outs = (o_hbm, gq_hbm, gk_hbm, gv_hbm)

    def out_src(kind, h, block):
        if kind == 0:
            return obuf.at[h, block]
        if kind == 1:
            return qgbuf.at[h, block]
        return fbuf.at[h, kind - 2, block]

    out_widths = (2 * HD, 2 * HD, HD, HD)

    def local_out(kind, h):
        return pltpu.make_async_copy(
            out_src(kind, h, core), outs[kind].at[0, :, cols(core, h, out_widths[kind])], ol_sem.at[kind, h])

    def partner_out(kind, h):
        return remote(
            out_src(kind, h, other), outs[kind].at[0, :, cols(core, h, out_widths[kind])],
            os_sem.at[kind, h], or_sem.at[kind, h], partner)

    def partner_out_recv(kind, h):
        return remote(
            out_src(kind, h, other), outs[kind].at[0, :, cols(other, h, out_widths[kind])],
            os_sem.at[kind, h], or_sem.at[kind, h], partner)

    def grad_send(h):
        return remote(gtx.at[h], grx.at[h], gs_sem.at[h], gr_sem.at[h], me - 2)

    def scale_send(h):
        return remote(stx.at[h], srx.at[h], ss_sem.at[h], sr_sem.at[h], me - 2)

    def head_step(h, terms):
        q_term, k_term = terms
        for kind in range(4):
            local_in(kind, h).wait()
            partner_in_recv(kind, h).wait_recv()

        @pl.when(has_prev)
        def _():
            for s in range(2):
                for kv in range(2):
                    halo_recv(s, kv, h).wait_recv()

        low = (lax.broadcasted_iota(jnp.int32, (2 * tok, tok), 1)
               <= lax.rem(lax.broadcasted_iota(jnp.int32, (2 * tok, tok), 0), tok))
        kx = kbuf[h].astype(F32)
        k_unit = kx * inv_rms(kx)
        kn = (k_unit * k_gain).astype(BF16)
        vv = vbuf[h]
        dks, dvs = [], []
        for blk in range(2):
            ks = slice(blk * tok, blk * tok + 3 * tok)
            out, gq, dk, dv, term = unit_step(
                qbuf[h, blk], dbuf[h, blk], kn[ks], vv[ks], bias[blk, 0], bias[blk, 1], low, q_gain)
            q_term = q_term + term
            obuf[h, blk, :, :HD] = out[:tok]
            obuf[h, blk, :, HD:] = out[tok:]
            qgbuf[h, blk, :, :HD] = gq[:tok]
            qgbuf[h, blk, :, HD:] = gq[tok:]
            dks.append(dk)
            dvs.append(dv)
        for kv, (a, b) in enumerate((dks, dvs)):
            for blk, grad in enumerate((a[:tok], a[tok:2 * tok] + b[:tok])):
                top = jnp.maximum(jnp.max(jnp.abs(grad), axis=-1, keepdims=True), 1e-30)
                gtx[h, kv, pl.ds(blk * tok, tok)] = (
                    jnp.round(grad * (CODE / top)).astype(jnp.int32).astype(jnp.int16))
                stx[h, pl.ds(2 * kv + blk, 1)] = jnp.transpose(
                    jnp.broadcast_to(top * (1.0 / CODE), (tok, tok)))[:1]
            own[h, kv, pl.ds(0, tok)] = a[2 * tok:] + b[tok:2 * tok]
            own[h, kv, pl.ds(tok, tok)] = b[2 * tok:]

        @pl.when(has_prev)
        def _():
            scale_send(h).start()
            grad_send(h).start()

        for kind in range(2):
            local_out(kind, h).start()
            partner_out(kind, h).start()
        a, b = dks
        for rows_of, grad in (
            (slice(0, tok), a[:tok]),
            (slice(tok, 2 * tok), a[tok:2 * tok] + b[:tok]),
            (slice(2 * tok, 3 * tok), a[2 * tok:] + b[tok:2 * tok]),
            (slice(3 * tok, 4 * tok), b[2 * tok:]),
        ):
            k_term = k_term + jnp.sum(grad * k_unit[rows_of], axis=0, keepdims=True)
        return q_term, k_term

    zero_row = jnp.zeros((1, HD), F32)
    q_term, k_term = lax.fori_loop(0, heads, head_step, (zero_row, zero_row))

    def final_step(h):
        @pl.when(has_next)
        def _():
            scale_send(h).wait_recv()
            grad_send(h).wait_recv()
        gk, gv = [
            jnp.concatenate([
                own[h, kv, pl.ds(blk * tok, tok)]
                + grx[h, kv, pl.ds(blk * tok, tok)].astype(jnp.int32).astype(F32)
                * jnp.transpose(jnp.broadcast_to(srx[h, pl.ds(2 * kv + blk, 1)], (tok, tok)))
                for blk in range(2)], axis=0)
            for kv in range(2)]
        kx = kbuf[h, pl.ds(2 * tok, 2 * tok)].astype(F32)
        inv = inv_rms(kx)
        unit = kx * inv
        gkb = norm_back(gk, unit, inv, k_gain).astype(BF16)
        gvb = gv.astype(BF16)
        for blk in range(2):
            fbuf[h, 0, blk] = gkb[blk * tok:(blk + 1) * tok]
            fbuf[h, 1, blk] = gvb[blk * tok:(blk + 1) * tok]
        for kind in (2, 3):
            partner_out(kind, h).start()
            local_out(kind, h).start()

    def term_copy(i):
        axis, bit, index = hops[i]
        return pltpu.make_async_remote_copy(
            src_ref=gall.at[i], dst_ref=gdp.at[i], send_sem=as_sem.at[i], recv_sem=ar_sem.at[i],
            device_id={axis: flip(index, bit)}, device_id_type=pl.DeviceIdType.MESH)

    gall[0] = jnp.concatenate([q_term, k_term], axis=0)
    term_copy(0).start()
    waits = [i * heads // len(hops) for i in range(len(hops))]
    for h in range(heads):
        final_step(h)
        for i, at in enumerate(waits):
            if at == h:
                term_copy(i).wait_recv()
                gall[i + 1] = gall[i] + gdp[i]
                if i + 1 < len(hops):
                    term_copy(i + 1).start()
    gain_ref[...] = gall[len(hops)] * (n_seq * n_dp * tok) ** (-0.5)

    def drain(h, carry):
        for kind in range(4):
            partner_in(kind, h).wait_send()
            local_out(kind, h).wait()
            partner_out(kind, h).wait_send()
            partner_out_recv(kind, h).wait_recv()

        @pl.when(has_next)
        def _():
            for t in range(2):
                for kv in range(2):
                    halo_send(t, kv, h).wait_send()

        @pl.when(has_prev)
        def _():
            grad_send(h).wait_send()
            scale_send(h).wait_send()
        return carry

    lax.fori_loop(0, heads, drain, 0)
    seg_partner.wait_send()

    @pl.when(has_next)
    def _():
        for t in range(2):
            seg_send(t).wait_send()

    for i in range(len(hops)):
        term_copy(i).wait_send()


def place(*refs):
    sem = refs[10]
    copies = [pltpu.make_async_copy(refs[i], refs[5 + i], sem.at[i]) for i in range(5)]
    for copy in copies:
        copy.start()
    for copy in copies:
        copy.wait()


def per_device(n_seq, n_dp, queries, keys, values, segments, q_gain, k_gain, d_attn):
    tok = queries.shape[1]
    assert tok == HD and WINDOW == 2 * tok
    heads = keys.shape[2] // HD // 2
    n_hops = n_seq.bit_length() + n_dp.bit_length() - 2
    assert n_seq & (n_seq - 1) == 0 and n_dp & (n_dp - 1) == 0 and n_seq >= 4
    any_spec = pl.BlockSpec(memory_space=pl.ANY)
    vmem = pl.BlockSpec(memory_space=pltpu.VMEM)
    dma = pltpu.SemaphoreType.DMA
    shape = jax.ShapeDtypeStruct
    queries, keys, values, segments, d_attn = (
        pltpu.with_memory_space_constraint(x, pltpu.HBM) for x in (queries, keys, values, segments, d_attn))
    results = pl.pallas_call(
        functools.partial(kernel, n_seq, n_dp, heads),
        out_shape=(
            shape(queries.shape, BF16), shape(queries.shape, BF16),
            shape(keys.shape, BF16), shape(keys.shape, BF16), shape((2, HD), F32),
        ),
        in_specs=[pl.BlockSpec(memory_space=pltpu.HBM)] * 5 + [vmem] * 2,
        out_specs=(any_spec,) * 4 + (vmem,),
        scratch_shapes=[
            pltpu.VMEM((heads, 2, tok, 2 * HD), BF16),
            pltpu.VMEM((heads, 2, tok, 2 * HD), BF16),
            pltpu.VMEM((heads, 4 * tok, HD), BF16),
            pltpu.VMEM((heads, 4 * tok, HD), BF16),
            pltpu.VMEM((4, 1, tok), jnp.int32),
            pltpu.VMEM((2, 2, 2 * tok, tok), F32),
            pltpu.VMEM((heads, 2, 2 * tok, HD), jnp.int16),
            pltpu.VMEM((heads, 2, 2 * tok, HD), jnp.int16),
            pltpu.VMEM((heads, 4, tok), F32),
            pltpu.VMEM((heads, 4, tok), F32),
            pltpu.VMEM((heads, 2, 2 * tok, HD), F32),
            pltpu.VMEM((heads, 2, tok, 2 * HD), BF16),
            pltpu.VMEM((heads, 2, tok, 2 * HD), BF16),
            pltpu.VMEM((heads, 2, 2, tok, HD), BF16),
            pltpu.VMEM((n_hops + 1, 2, HD), F32),
            pltpu.VMEM((n_hops, 2, HD), F32),
            dma((4, heads)), dma((4, heads)), dma((4, heads)),
            dma((2, 2, heads)), dma((2, 2, heads)),
            dma((1,)), dma((1,)), dma((1,)), dma((2,)), dma((2,)),
            dma((heads,)), dma((heads,)), dma((heads,)), dma((heads,)),
            dma((4, heads)), dma((4, heads)), dma((4, heads)),
            dma((n_hops,)), dma((n_hops,)),
        ],
        compiler_params=pltpu.CompilerParams(
            collective_id=0, has_side_effects=True, vmem_limit_bytes=40 << 20),
    )(queries, keys, values, segments, d_attn, q_gain.reshape(1, HD), k_gain.reshape(1, HD))
    return pl.pallas_call(
        place,
        out_shape=tuple(shape(x.shape, x.dtype) for x in results),
        in_specs=[vmem] * 5,
        out_specs=(any_spec,) * 5,
        scratch_shapes=[dma((5,))],
        compiler_params=pltpu.CompilerParams(vmem_limit_bytes=50 << 20),
    )(*results)


def solution(mesh):
    tokens = P("dp", "seq", None)
    return jax.shard_map(
        functools.partial(per_device, mesh.shape["seq"], mesh.shape["dp"]),
        mesh=mesh,
        in_specs=(tokens, tokens, tokens, P("dp", "seq"), P(), P(), tokens),
        out_specs=(tokens, tokens, tokens, tokens, P()),
        check_vma=False,
    )
```

```python
import functools
import math

import jax
import jax.numpy as jnp
from jax import lax
from jax.experimental import pallas as pl
from jax.experimental.pallas import tpu as pltpu
from jax.sharding import PartitionSpec as P

QPA = 168
WINDOW = 256
HD = 128
EPS = 1e-06
SCALE = QPA ** (-0.5)
EXP2_SCALE = SCALE * math.log2(math.e)
CODE = 32767.0
F32 = jnp.float32
BF16 = jnp.bfloat16


def dot(a, b, ca, cb):
    return lax.dot_general(a, b, (((ca,), (cb,)), ((), ())), preferred_element_type=F32)


def inv_rms(x):
    return 1.0 / jnp.sqrt(jnp.mean(x * x, axis=-1, keepdims=True) + EPS)


def stack_heads(x):
    return jnp.concatenate([x[:, :HD], x[:, HD:]], axis=0)


def norm_back(grad, unit, inv, gain):
    t = grad * gain
    return (t - unit * jnp.mean(t * unit, axis=-1, keepdims=True)) * inv


def unit_step(q_raw, c_raw, kn, v, bias02, bias1, low, q_gain):
    x = stack_heads(q_raw).astype(F32)
    c = stack_heads(c_raw)
    inv = inv_rms(x)
    unit = x * inv
    qn = (unit * q_gain).astype(BF16)
    s = dot(qn, kn, 1, 1)
    gp = dot(c, v, 1, 1)
    n = HD
    x02 = jnp.where(low, s[:, 2 * n:], s[:, :n]) + bias02
    x1 = s[:, n:2 * n] + bias1
    m = jnp.max(jnp.maximum(x02, x1), axis=-1, keepdims=True)
    e02 = jnp.exp2((x02 - m) * EXP2_SCALE)
    e1 = jnp.exp2((x1 - m) * EXP2_SCALE)
    il = 1.0 / jnp.sum(e02 + e1, axis=-1, keepdims=True)
    p02 = e02 * il
    p1 = e1 * il
    g02 = jnp.where(low, gp[:, 2 * n:], gp[:, :n])
    g1 = gp[:, n:2 * n]
    rd = jnp.sum(p02 * g02 + p1 * g1, axis=-1, keepdims=True)
    d02 = p02 * (g02 - rd) * SCALE
    d1 = p1 * (g1 - rd) * SCALE

    def spread(a02, a1):
        return jnp.concatenate(
            [jnp.where(low, 0.0, a02).astype(BF16), a1.astype(BF16), jnp.where(low, a02, 0.0).astype(BF16)],
            axis=1,
        )

    plow = spread(p02, p1)
    gs = spread(d02, d1)
    out = dot(plow, v, 1, 0)
    dq = dot(gs, kn, 1, 0)
    dk = dot(gs, qn, 0, 0)
    dv = dot(plow, c, 0, 0)
    gq = norm_back(dq, unit, inv, q_gain)
    return out.astype(BF16), gq.astype(BF16), dk, dv, jnp.sum(dq * unit, axis=0, keepdims=True)


def kernel(
    n_seq, n_dp, heads,
    q_hbm, k_hbm, v_hbm, seg_hbm, d_hbm, qg_ref, kg_ref,
    o_hbm, gq_hbm, gk_hbm, gv_hbm, gain_ref,
    qbuf, dbuf, kbuf, vbuf, sbuf, bias, gtx, grx, stx, srx, own, obuf, qgbuf, fbuf, gall,
    loc_sem, ps_sem, pr_sem, hs_sem, hr_sem, sls, sps, spr, shs, shr,
    gs_sem, gr_sem, ss_sem, sr_sem, ol_sem, os_sem, or_sem, as_sem, ar_sem,
):
    me = lax.axis_index("seq")
    my_dp = lax.axis_index("dp")
    core = lax.rem(me, 2)
    other = 1 - core
    partner = me + 1 - 2 * core
    first = me - core
    has_prev = first >= 2
    has_next = first + 2 < n_seq
    tok = HD

    def cols(half, h, width):
        return pl.ds(pl.multiple_of((half * heads + h) * width, width), width)

    def rows(block):
        return pl.ds(pl.multiple_of(block * tok, tok), tok)

    def remote(src, dst, ss, rs, dev):
        return pltpu.make_async_remote_copy(
            src_ref=src, dst_ref=dst, send_sem=ss, recv_sem=rs,
            device_id={"seq": dev}, device_id_type=pl.DeviceIdType.MESH,
        )

    ins = (q_hbm, k_hbm, v_hbm, d_hbm)
    widths = (2 * HD, HD, HD, 2 * HD)

    def in_dst(kind, h, block):
        if kind == 0:
            return qbuf.at[h, block]
        if kind == 3:
            return dbuf.at[h, block]
        return (kbuf if kind == 1 else vbuf).at[h, rows(2 + block)]

    def local_in(kind, h):
        return pltpu.make_async_copy(
            ins[kind].at[0, :, cols(core, h, widths[kind])], in_dst(kind, h, core), loc_sem.at[kind, h])

    def partner_in(kind, h):
        return remote(
            ins[kind].at[0, :, cols(other, h, widths[kind])], in_dst(kind, h, core),
            ps_sem.at[kind, h], pr_sem.at[kind, h], partner)

    def partner_in_recv(kind, h):
        return remote(
            ins[kind].at[0, :, cols(core, h, widths[kind])], in_dst(kind, h, other),
            ps_sem.at[kind, h], pr_sem.at[kind, h], partner)

    def halo_send(t, kv, h):
        return remote(
            ins[1 + kv].at[0, :, cols(t, h, HD)], (kbuf, vbuf)[kv].at[h, rows(core)],
            hs_sem.at[t, kv, h], hr_sem.at[core, kv, h], first + 2 + t)

    def halo_recv(s, kv, h):
        return remote(
            ins[1 + kv].at[0, :, cols(core, h, HD)], (kbuf, vbuf)[kv].at[h, pl.ds(s * tok, tok)],
            hs_sem.at[s, kv, h], hr_sem.at[s, kv, h], partner)

    def seg_send(t):
        return remote(seg_hbm, sbuf.at[core], shs.at[t], shr.at[core], first + 2 + t)

    def seg_recv(s):
        return remote(seg_hbm, sbuf.at[s], shs.at[s], shr.at[s], partner)

    seg_local = pltpu.make_async_copy(seg_hbm, sbuf.at[2 + core], sls.at[0])
    seg_partner = remote(seg_hbm, sbuf.at[2 + core], sps.at[0], spr.at[0], partner)
    seg_partner_recv = remote(seg_hbm, sbuf.at[2 + other], sps.at[0], spr.at[0], partner)

    barrier = pltpu.get_barrier_semaphore()

    def greet(axis, dev):
        pl.semaphore_signal(barrier, inc=1, device_id={axis: dev}, device_id_type=pl.DeviceIdType.MESH)

    bits = [("seq", 1 << i) for i in range(n_seq.bit_length() - 1)]
    bits += [("dp", 1 << i) for i in range(n_dp.bit_length() - 1)]
    groups = [bits[i:i + 3] for i in range(0, len(bits), 3)]
    at = {"seq": me, "dp": my_dp}

    def bit_of(axis, bit):
        return lax.rem(at[axis] // bit, 2)

    def coordinate(group, mask):
        total = 0
        for j, (axis, bit) in enumerate(group):
            mine = bit_of(axis, bit)
            total = total + ((1 - mine) if mask >> j & 1 else mine) * (1 << j)
        return total

    def peer(group, mask):
        where = dict(at)
        for j, (axis, bit) in enumerate(group):
            if mask >> j & 1:
                where[axis] = where[axis] + bit - 2 * bit * bit_of(axis, bit)
        return where

    greeted = 0
    for group in groups:
        for mask in range(1, 1 << len(group)):
            greeted += 1
            pl.semaphore_signal(barrier, inc=1, device_id=peer(group, mask),
                                device_id_type=pl.DeviceIdType.MESH)

    @pl.when(has_next)
    def _():
        greet("seq", first + 2)
        greet("seq", first + 3)

    @pl.when(has_prev)
    def _():
        greet("seq", first - 2)
        greet("seq", first - 1)


    seg_local.start()
    for h in range(heads):
        for kind in range(4):
            local_in(kind, h).start()

    @pl.when(jnp.logical_not(has_prev))
    def _():
        for h in range(heads):
            kbuf[h, pl.ds(0, 2 * tok)] = jnp.zeros((2 * tok, HD), BF16)
            vbuf[h, pl.ds(0, 2 * tok)] = jnp.zeros((2 * tok, HD), BF16)
        sbuf[0] = jnp.full((1, tok), -1, jnp.int32)
        sbuf[1] = jnp.full((1, tok), -1, jnp.int32)

    @pl.when(jnp.logical_not(has_next))
    def _():
        for h in range(heads):
            for kv in range(2):
                grx[h, kv] = jnp.zeros((2 * tok, HD), jnp.int16)
            srx[h] = jnp.zeros((4, tok), F32)

    pl.semaphore_wait(barrier, greeted + 2 * has_prev.astype(jnp.int32) + 2 * has_next.astype(jnp.int32))

    seg_partner.start()

    @pl.when(has_next)
    def _():
        for t in range(2):
            seg_send(t).start()

    for h in range(heads):
        @pl.when(has_next)
        def _():
            for t in range(2):
                for kv in range(2):
                    halo_send(t, kv, h).start()
        for kind in range(4):
            partner_in(kind, h).start()

    seg_local.wait()
    seg_partner_recv.wait_recv()

    @pl.when(has_prev)
    def _():
        for s in range(2):
            seg_recv(s).wait_recv()

    row_i = lax.broadcasted_iota(jnp.int32, (tok, tok), 0)
    col_i = lax.broadcasted_iota(jnp.int32, (tok, tok), 1)
    lower = col_i <= row_i
    docs = [jnp.broadcast_to(sbuf[i], (tok, tok)) for i in range(4)]
    for blk in range(2):
        mine = jnp.transpose(docs[blk + 2])
        b02 = jnp.where(mine == jnp.where(lower, docs[blk + 2], docs[blk]), 0.0, -1e30)
        b1 = jnp.where(mine == docs[blk + 1], 0.0, -1e30)
        for half in range(2):
            bias[blk, 0, pl.ds(half * tok, tok)] = b02
            bias[blk, 1, pl.ds(half * tok, tok)] = b1

    q_gain = qg_ref[...]
    k_gain = kg_ref[...]

    outs = (o_hbm, gq_hbm, gk_hbm, gv_hbm)

    def out_src(kind, h, block):
        if kind == 0:
            return obuf.at[h, block]
        if kind == 1:
            return qgbuf.at[h, block]
        return fbuf.at[h, kind - 2, block]

    out_widths = (2 * HD, 2 * HD, HD, HD)

    def local_out(kind, h):
        return pltpu.make_async_copy(
            out_src(kind, h, core), outs[kind].at[0, :, cols(core, h, out_widths[kind])], ol_sem.at[kind, h])

    def partner_out(kind, h):
        return remote(
            out_src(kind, h, other), outs[kind].at[0, :, cols(core, h, out_widths[kind])],
            os_sem.at[kind, h], or_sem.at[kind, h], partner)

    def partner_out_recv(kind, h):
        return remote(
            out_src(kind, h, other), outs[kind].at[0, :, cols(other, h, out_widths[kind])],
            os_sem.at[kind, h], or_sem.at[kind, h], partner)

    def grad_send(h):
        return remote(gtx.at[h], grx.at[h], gs_sem.at[h], gr_sem.at[h], me - 2)

    def scale_send(h):
        return remote(stx.at[h], srx.at[h], ss_sem.at[h], sr_sem.at[h], me - 2)

    def head_step(h, terms):
        q_term, k_term = terms
        for kind in range(4):
            local_in(kind, h).wait()
            partner_in_recv(kind, h).wait_recv()

        @pl.when(has_prev)
        def _():
            for s in range(2):
                for kv in range(2):
                    halo_recv(s, kv, h).wait_recv()

        low = (lax.broadcasted_iota(jnp.int32, (2 * tok, tok), 1)
               <= lax.rem(lax.broadcasted_iota(jnp.int32, (2 * tok, tok), 0), tok))
        kx = kbuf[h].astype(F32)
        k_unit = kx * inv_rms(kx)
        kn = (k_unit * k_gain).astype(BF16)
        vv = vbuf[h]
        dks, dvs = [], []
        for blk in range(2):
            ks = slice(blk * tok, blk * tok + 3 * tok)
            out, gq, dk, dv, term = unit_step(
                qbuf[h, blk], dbuf[h, blk], kn[ks], vv[ks], bias[blk, 0], bias[blk, 1], low, q_gain)
            q_term = q_term + term
            obuf[h, blk, :, :HD] = out[:tok]
            obuf[h, blk, :, HD:] = out[tok:]
            qgbuf[h, blk, :, :HD] = gq[:tok]
            qgbuf[h, blk, :, HD:] = gq[tok:]
            dks.append(dk)
            dvs.append(dv)
        for kv, (a, b) in enumerate((dks, dvs)):
            for blk, grad in enumerate((a[:tok], a[tok:2 * tok] + b[:tok])):
                top = jnp.maximum(jnp.max(jnp.abs(grad), axis=-1, keepdims=True), 1e-30)
                gtx[h, kv, pl.ds(blk * tok, tok)] = (
                    jnp.round(grad * (CODE / top)).astype(jnp.int32).astype(jnp.int16))
                stx[h, pl.ds(2 * kv + blk, 1)] = jnp.transpose(
                    jnp.broadcast_to(top * (1.0 / CODE), (tok, tok)))[:1]
            own[h, kv, pl.ds(0, tok)] = a[2 * tok:] + b[tok:2 * tok]
            own[h, kv, pl.ds(tok, tok)] = b[2 * tok:]

        @pl.when(has_prev)
        def _():
            scale_send(h).start()
            grad_send(h).start()

        for kind in range(2):
            local_out(kind, h).start()
            partner_out(kind, h).start()
        a, b = dks
        for rows_of, grad in (
            (slice(0, tok), a[:tok]),
            (slice(tok, 2 * tok), a[tok:2 * tok] + b[:tok]),
            (slice(2 * tok, 3 * tok), a[2 * tok:] + b[tok:2 * tok]),
            (slice(3 * tok, 4 * tok), b[2 * tok:]),
        ):
            k_term = k_term + jnp.sum(grad * k_unit[rows_of], axis=0, keepdims=True)
        return q_term, k_term

    zero_row = jnp.zeros((1, HD), F32)
    q_term, k_term = lax.fori_loop(0, heads, head_step, (zero_row, zero_row))

    def final_step(h):
        @pl.when(has_next)
        def _():
            scale_send(h).wait_recv()
            grad_send(h).wait_recv()
        gk, gv = [
            jnp.concatenate([
                own[h, kv, pl.ds(blk * tok, tok)]
                + grx[h, kv, pl.ds(blk * tok, tok)].astype(jnp.int32).astype(F32)
                * jnp.transpose(jnp.broadcast_to(srx[h, pl.ds(2 * kv + blk, 1)], (tok, tok)))
                for blk in range(2)], axis=0)
            for kv in range(2)]
        kx = kbuf[h, pl.ds(2 * tok, 2 * tok)].astype(F32)
        inv = inv_rms(kx)
        unit = kx * inv
        gkb = norm_back(gk, unit, inv, k_gain).astype(BF16)
        gvb = gv.astype(BF16)
        for blk in range(2):
            fbuf[h, 0, blk] = gkb[blk * tok:(blk + 1) * tok]
            fbuf[h, 1, blk] = gvb[blk * tok:(blk + 1) * tok]
        for kind in (2, 3):
            partner_out(kind, h).start()
            local_out(kind, h).start()

    def term_copy(g, mask, slot):
        return pltpu.make_async_remote_copy(
            src_ref=gall.at[g, slot], dst_ref=gall.at[g, slot],
            send_sem=as_sem.at[g, mask], recv_sem=ar_sem.at[g, mask],
            device_id=peer(groups[g], mask), device_id_type=pl.DeviceIdType.MESH)

    def masks(g):
        return range(1, 1 << len(groups[g]))

    def share(g, value):
        mine = coordinate(groups[g], 0)
        gall[g, mine] = value
        for mask in masks(g):
            term_copy(g, mask, mine).start()

    def collect(g):
        for mask in masks(g):
            term_copy(g, mask, coordinate(groups[g], mask)).wait_recv()
        total = gall[g, 0]
        for slot in range(1, 1 << len(groups[g])):
            total = total + gall[g, slot]
        return total

    share(0, jnp.concatenate([q_term, k_term], axis=0))
    for h in range(heads - 1):
        final_step(h)
    for g in range(len(groups)):
        total = collect(g)
        if g + 1 < len(groups):
            share(g + 1, total)
        if g == 0:
            final_step(heads - 1)
    gain_ref[...] = total * (n_seq * n_dp * tok) ** (-0.5)

    def drain(h, carry):
        for kind in range(4):
            partner_in(kind, h).wait_send()
            local_out(kind, h).wait()
            partner_out(kind, h).wait_send()
            partner_out_recv(kind, h).wait_recv()

        @pl.when(has_next)
        def _():
            for t in range(2):
                for kv in range(2):
                    halo_send(t, kv, h).wait_send()

        @pl.when(has_prev)
        def _():
            grad_send(h).wait_send()
            scale_send(h).wait_send()
        return carry

    lax.fori_loop(0, heads, drain, 0)
    seg_partner.wait_send()

    @pl.when(has_next)
    def _():
        for t in range(2):
            seg_send(t).wait_send()

    for g in range(len(groups)):
        for mask in masks(g):
            term_copy(g, mask, coordinate(groups[g], 0)).wait_send()


def place(*refs):
    sem = refs[10]
    copies = [pltpu.make_async_copy(refs[i], refs[5 + i], sem.at[i]) for i in range(5)]
    for copy in copies:
        copy.start()
    for copy in copies:
        copy.wait()


def per_device(n_seq, n_dp, queries, keys, values, segments, q_gain, k_gain, d_attn):
    tok = queries.shape[1]
    assert tok == HD and WINDOW == 2 * tok
    heads = keys.shape[2] // HD // 2
    n_groups = (n_seq.bit_length() + n_dp.bit_length()) // 3
    assert n_seq & (n_seq - 1) == 0 and n_dp & (n_dp - 1) == 0 and n_seq >= 4
    any_spec = pl.BlockSpec(memory_space=pl.ANY)
    vmem = pl.BlockSpec(memory_space=pltpu.VMEM)
    dma = pltpu.SemaphoreType.DMA
    shape = jax.ShapeDtypeStruct
    queries, keys, values, segments, d_attn = (
        pltpu.with_memory_space_constraint(x, pltpu.HBM) for x in (queries, keys, values, segments, d_attn))
    results = pl.pallas_call(
        functools.partial(kernel, n_seq, n_dp, heads),
        out_shape=(
            shape(queries.shape, BF16), shape(queries.shape, BF16),
            shape(keys.shape, BF16), shape(keys.shape, BF16), shape((2, HD), F32),
        ),
        in_specs=[pl.BlockSpec(memory_space=pltpu.HBM)] * 5 + [vmem] * 2,
        out_specs=(any_spec,) * 4 + (vmem,),
        scratch_shapes=[
            pltpu.VMEM((heads, 2, tok, 2 * HD), BF16),
            pltpu.VMEM((heads, 2, tok, 2 * HD), BF16),
            pltpu.VMEM((heads, 4 * tok, HD), BF16),
            pltpu.VMEM((heads, 4 * tok, HD), BF16),
            pltpu.VMEM((4, 1, tok), jnp.int32),
            pltpu.VMEM((2, 2, 2 * tok, tok), F32),
            pltpu.VMEM((heads, 2, 2 * tok, HD), jnp.int16),
            pltpu.VMEM((heads, 2, 2 * tok, HD), jnp.int16),
            pltpu.VMEM((heads, 4, tok), F32),
            pltpu.VMEM((heads, 4, tok), F32),
            pltpu.VMEM((heads, 2, 2 * tok, HD), F32),
            pltpu.VMEM((heads, 2, tok, 2 * HD), BF16),
            pltpu.VMEM((heads, 2, tok, 2 * HD), BF16),
            pltpu.VMEM((heads, 2, 2, tok, HD), BF16),
            pltpu.VMEM((n_groups, 8, 2, HD), F32),
            dma((4, heads)), dma((4, heads)), dma((4, heads)),
            dma((2, 2, heads)), dma((2, 2, heads)),
            dma((1,)), dma((1,)), dma((1,)), dma((2,)), dma((2,)),
            dma((heads,)), dma((heads,)), dma((heads,)), dma((heads,)),
            dma((4, heads)), dma((4, heads)), dma((4, heads)),
            dma((n_groups, 8)), dma((n_groups, 8)),
        ],
        compiler_params=pltpu.CompilerParams(
            collective_id=0, has_side_effects=True, vmem_limit_bytes=40 << 20),
    )(queries, keys, values, segments, d_attn, q_gain.reshape(1, HD), k_gain.reshape(1, HD))
    return pl.pallas_call(
        place,
        out_shape=tuple(shape(x.shape, x.dtype) for x in results),
        in_specs=[vmem] * 5,
        out_specs=(any_spec,) * 5,
        scratch_shapes=[dma((5,))],
        compiler_params=pltpu.CompilerParams(vmem_limit_bytes=50 << 20),
    )(*results)


def solution(mesh):
    tokens = P("dp", "seq", None)
    return jax.shard_map(
        functools.partial(per_device, mesh.shape["seq"], mesh.shape["dp"]),
        mesh=mesh,
        in_specs=(tokens, tokens, tokens, P("dp", "seq"), P(), P(), tokens),
        out_specs=(tokens, tokens, tokens, tokens, P()),
        check_vma=False,
    )
```
